32 devices in a mesh: segment: 2 (over x), seq: 4 (over z), tp: 4 (over y, core).
Axes of the slice: x: 2, y: 2, z: 4, core: 2. Of those that a mesh axis runs over, the one named last changes fastest.
Arguments:
- queries: bfloat16 [2, 1024, 4096], P('segment', ('seq', 'tp')), may hold values from -64 to 64
- key_rows: bfloat16 [2, 1024, 4096], P('segment', 'seq'), may hold values from -64 to 64
- value_rows: bfloat16 [2, 1024, 4096], P('segment', 'seq'), may hold values from -6 to 6
- mod_scale: float32 [2, 4096], P('segment'), may hold values from -3 to 3
- mod_shift: float32 [2, 4096], P('segment'), may hold values from -3 to 3
- head_weight: bfloat16 [4096, 64], replicated, may hold values from -0.09375 to 0.09375
- tile_lists: int32 [16, 32], P('seq'), may hold values from 0 to 128, as said below
- latent_mean: float32 [16], replicated, may hold values from -4 to 4
- latent_std: float32 [16], replicated, may hold values from 0.5 to 3
- conv_weight: bfloat16 [432, 384], replicated, may hold values from -0.3125 to 0.3125
- conv_bias: float32 [384], replicated, may hold values from -3 to 3
Outputs:
- latents: bfloat16 [2, 1024, 64], P('segment', ('seq', 'tp'))
- decoded: bfloat16 [2, 16, 8, 128, 384], P('segment', 'seq', 'tp')
The draws below stay inside these ranges and needn't reach their ends.
Inputs may be any that keep to these rules, and one draw needn't show every extreme that they name: `tile_lists`: each tile is a 4 x 8 window of patches at some anchor, possibly partly outside the frame; every owner's list has the same length.
All inputs are finite; a program needn't handle non-finite values.
Results may differ from the reference program's by a relative error of at most 0.0068.
Values may be sent and summed in bfloat16 or wider, within the bound.
No kernel may reach another device: no remote copies, remote signals or barrier semaphores. Data moves between devices by JAX's collectives and lax.ppermute only.
A program may use at most 128 MiB of HBM per device.

```python
import math
import jax
import jax.numpy as jnp
from jax import lax

HEADS = 32
HD = 128
HC = 4096
LAT = 16
PATCHC = 64
VCH = 384
CT = 2
WP = 32
TH = 4
TW = 8
TILE_P = 32
HP = 4
SP = 128
LT = 8
TOKENS = 1024
TILES = 16
N_SEQ = 4
N_TP = 4


def keys_common(key):
    base = jax.random.normal(jax.random.fold_in(key, 7), (2, TOKENS, HC), jnp.float32)
    return base


def draw_key_rows(key, part):
    return keys_common(key).astype(jnp.bfloat16)


def draw_queries(key, part):
    base = jax.random.normal(jax.random.fold_in(key, 3), (2, TOKENS, HC), jnp.float32)
    return base.astype(jnp.bfloat16)


def draw_tile_lists(key, part):
    row_anchor = jax.random.randint(jax.random.fold_in(key, 21), (TILES,), -1, HP - TH + 2)
    col_anchor = jax.random.randint(jax.random.fold_in(key, 22), (TILES,), -2, WP - TW + 3)
    first = jnp.arange(TILES) == 0
    row_anchor = jnp.where(first, -1, row_anchor)
    col_anchor = jnp.where(first, -2, col_anchor)
    inner = jnp.arange(TILE_P)
    rows_at = row_anchor[:, None] + inner[None, :] // TW
    cols_at = col_anchor[:, None] + inner[None, :] % TW
    inside = (rows_at >= 0) & (rows_at < HP) & (cols_at >= 0) & (cols_at < WP)
    return jnp.where(inside, rows_at * WP + cols_at, SP).astype(jnp.int32)


def levels(key, dims, cuts, least, largest):
    level = 1.0
    for dim, shards_of in cuts:
        steps = jax.random.uniform(jax.random.fold_in(jax.random.fold_in(key, 6), dim), (shards_of,), jnp.float32, least / len(cuts), largest / len(cuts))
        level = level * jnp.repeat(jnp.exp(steps), dims[dim] // shards_of).reshape((-1,) + (1,) * (len(dims) - 1 - dim))
    return level


def centred(own_key, shape, width, bound, pieces=(), dtype=jnp.bfloat16):
    values = jax.random.normal(own_key, shape, jnp.float32) * width
    if len(pieces) > 0:
        values = levels(own_key, shape, pieces, -0.22, 0.18) * values
    return jnp.clip(values, min=-bound, max=bound).astype(dtype)


def setup_inputs(seed: int = 0) -> dict:
    key_of = jax.random.split(jax.random.key(seed), 12)
    return {
        "queries": draw_queries(jax.random.fold_in(key_of[11], 71), 0),
        "key_rows": draw_key_rows(jax.random.fold_in(key_of[11], 71), 0),
        "value_rows": centred(key_of[2], (2, TOKENS, HC), 1.0, 6.0, ((0, 2), (1, 4))),
        "mod_scale": centred(key_of[3], (2, HC), 0.5, 3.0, ((0, 2),), jnp.float32),
        "mod_shift": centred(key_of[4], (2, HC), 0.5, 3.0, ((0, 2),), jnp.float32),
        "head_weight": centred(key_of[5], (HC, PATCHC), HC ** -0.5, 0.09375),
        "tile_lists": draw_tile_lists(jax.random.fold_in(key_of[11], 71), 0),
        "latent_mean": centred(key_of[7], (LAT,), 1.0, 4.0, (), jnp.float32),
        "latent_std": jnp.clip(jnp.exp(jax.random.uniform(key_of[8], (LAT,), jnp.float32, math.log(0.5), math.log(3.0))), 0.5, 3.0),
        "conv_weight": centred(key_of[9], (27 * LAT, VCH), (27 * LAT) ** -0.5, 0.3125),
        "conv_bias": centred(key_of[10], (VCH,), 0.5, 3.0, (), jnp.float32),
    }


epsilon = 1e-06

def convolve_frames(framed, out_frames, conv_weight, conv_bias):
    tiles_here = framed.shape[1]
    picture = framed.reshape(out_frames + 2, tiles_here, TH, TW, 2, 2, LAT)
    picture = picture.transpose(0, 1, 2, 4, 3, 5, 6).reshape(out_frames + 2, tiles_here, 2 * TH, 2 * TW, LAT)
    picture = jnp.pad(picture, ((0, 0), (0, 0), (1, 1), (1, 1), (0, 0)))
    columns = []
    for shift_t in range(3):
        for shift_y in range(3):
            for shift_x in range(3):
                columns.append(picture[shift_t:shift_t + out_frames, :, shift_y:shift_y + 2 * TH, shift_x:shift_x + 2 * TW, :])
    stacked = jnp.concatenate(columns, axis=-1).reshape(-1, 27 * LAT)
    result = jnp.dot(stacked, conv_weight, preferred_element_type=jnp.float32) + conv_bias
    return result.astype(jnp.bfloat16).reshape(out_frames, tiles_here, 4 * TH * TW, VCH)

def restore_latent(picked, tile_lists, patch_count, latent_mean, latent_std):
    inside = (tile_lists < patch_count)[None, :, :, None]
    spread = jnp.tile(latent_std, 4)
    centre = jnp.tile(latent_mean, 4)
    return jnp.where(inside, picked.astype(jnp.float32) * spread + centre, 0.0).astype(jnp.bfloat16)

def attend_head(query, key_part, value_part):
    span = math.gcd(TOKENS, 1024)

    def one_block(query_block):
        scores = jnp.dot(query_block, key_part.T, preferred_element_type=jnp.float32) * HD ** (-0.5)
        peak = lax.optimization_barrier(jnp.max(scores, axis=-1, keepdims=True))
        powers = jnp.exp(scores - peak)
        total = lax.optimization_barrier(jnp.sum(powers, axis=-1, keepdims=True))
        weights = (powers / total).astype(jnp.bfloat16)
        return jnp.dot(weights, value_part, preferred_element_type=jnp.float32).astype(jnp.bfloat16)
    return lax.map(one_block, query.reshape(TOKENS // span, span, HD)).reshape(TOKENS, HD)

def split_heads(array):
    return array.reshape(TOKENS, HEADS, HD).transpose(1, 0, 2)

def run_transformer(query, key_all, value_all, scale_row, shift_row, head_weight):
    mixed = lax.map(lambda triple: attend_head(triple[0], triple[1], triple[2]), (split_heads(query), split_heads(key_all), split_heads(value_all)))
    joined = mixed.transpose(1, 0, 2).reshape(TOKENS, HC).astype(jnp.float32)
    average = lax.optimization_barrier(jnp.mean(joined, axis=-1, keepdims=True))
    variance = lax.optimization_barrier(jnp.mean((joined - average) ** 2, axis=-1, keepdims=True))
    normed = (joined - average) * lax.rsqrt(variance + epsilon)
    hidden = (normed * (1.0 + scale_row) + shift_row).astype(jnp.bfloat16)
    return jnp.dot(hidden, head_weight, preferred_element_type=jnp.float32).astype(jnp.bfloat16)

def decode_video(latent, tile_lists, latent_mean, latent_std, conv_weight, conv_bias):
    grid = latent.reshape(N_SEQ, N_TP, CT, WP, PATCHC).transpose(1, 2, 0, 3, 4).reshape(LT, SP, PATCHC)
    grid = jnp.concatenate([grid, jnp.zeros((LT, 1, PATCHC), jnp.bfloat16)], axis=1)
    picked = jnp.take(grid, tile_lists.reshape(-1), axis=1).reshape(LT, TILES, TILE_P, PATCHC)
    framed = restore_latent(picked, tile_lists, SP, latent_mean, latent_std)
    framed = jnp.concatenate([jnp.zeros((2, TILES, TILE_P, PATCHC), jnp.bfloat16), framed], axis=0)
    result = convolve_frames(framed, LT, conv_weight, conv_bias)
    return result.transpose(1, 0, 2, 3)

def reference(queries, key_rows, value_rows, mod_scale, mod_shift, head_weight, tile_lists, latent_mean, latent_std, conv_weight, conv_bias):
    latents = jnp.stack([run_transformer(queries[video_index], key_rows[video_index], value_rows[video_index], mod_scale[video_index], mod_shift[video_index], head_weight) for video_index in range(2)])
    decoded = jnp.stack([decode_video(latents[1 - video_index], tile_lists, latent_mean, latent_std, conv_weight, conv_bias) for video_index in range(2)])
    return (latents, decoded)
```

```python
import functools
import math

import jax
import jax.numpy as jnp
from jax import lax
from jax.experimental import pallas as pl
from jax.experimental.pallas import tpu as pltpu
from jax.sharding import PartitionSpec as P

HD = 128
LAT = 16
PATCHC = 64
CT = 2
WP = 32
TH = 4
TW = 8
TILE_P = 32
PACK = 80

epsilon = 1e-06


NT = (((1,), (1,)), ((), ()))
TN = (((0,), (0,)), ((), ()))


def xor_permute(value, axis, mask):
    pairs = [(i, i ^ mask) for i in range(lax.axis_size(axis))]
    return lax.ppermute(value, axis, pairs)


def split3(value):
    high = value.astype(jnp.bfloat16)
    rest = value - high.astype(jnp.float32)
    middle = rest.astype(jnp.bfloat16)
    low = (rest - middle.astype(jnp.float32)).astype(jnp.bfloat16)
    return [high.astype(jnp.float32), middle.astype(jnp.float32), low.astype(jnp.float32)]


def scores_kernel(pieces, heads, q_ref, *refs):
    k_refs, (p_ref, l_ref) = refs[:pieces], refs[pieces:]
    factor = HD ** (-0.5) * math.log2(math.e)
    for head in range(heads):
        columns = slice(head * HD, (head + 1) * HD)
        query = q_ref[:, columns]
        scores = [
            lax.dot_general(k[:, columns], query, NT, preferred_element_type=jnp.float32)
            for k in k_refs
        ]
        peak = functools.reduce(jnp.maximum, [jnp.max(x, axis=0, keepdims=True) for x in scores])
        total = 0.0
        for i, x in enumerate(scores):
            powers = jnp.exp2((x - peak) * factor)
            total = total + jnp.sum(powers, axis=0, keepdims=True)
            rows = x.shape[0]
            p_ref[0, head, i * rows : (i + 1) * rows, :] = powers.astype(jnp.bfloat16)
        l_ref[0, head : head + 1, :] = total


def score_weights(query, key_pieces, block):
    rows, width = query.shape
    heads = width // HD
    keys = sum(k.shape[0] for k in key_pieces)
    blocks = rows // block
    return pl.pallas_call(
        functools.partial(scores_kernel, len(key_pieces), heads),
        grid=(blocks,),
        in_specs=[pl.BlockSpec((block, width), lambda i: (i, 0))]
        + [pl.BlockSpec(k.shape, lambda i: (0, 0)) for k in key_pieces],
        out_specs=[
            pl.BlockSpec((1, heads, keys, block), lambda i: (i, 0, 0, 0)),
            pl.BlockSpec((1, heads, block), lambda i: (i, 0, 0)),
        ],
        out_shape=[
            jax.ShapeDtypeStruct((blocks, heads, keys, block), jnp.bfloat16),
            jax.ShapeDtypeStruct((blocks, heads, block), jnp.float32),
        ],
        name="scores",
    )(query, *key_pieces)


def values_kernel(pieces, heads, p_ref, l_ref, scale_ref, w_ref, *refs):
    v_refs, out_ref = refs[:pieces], refs[pieces]
    rows = v_refs[0].shape[0]
    mixed = []
    for head in range(heads):
        columns = slice(head * HD, (head + 1) * HD)
        total = 0.0
        for i, v in enumerate(v_refs):
            total = total + lax.dot_general(
                v[:, columns],
                p_ref[0, head, i * rows : (i + 1) * rows, :],
                TN,
                preferred_element_type=jnp.float32,
            )
        total = total / l_ref[0, head : head + 1, :]
        mixed.append(total.astype(jnp.bfloat16).astype(jnp.float32))
    attended = jnp.concatenate(mixed, axis=0)
    width = attended.shape[0]
    average = jnp.sum(attended, axis=0, keepdims=True) * (1.0 / width)
    centred = attended - average
    squares = jnp.sum(centred * centred, axis=0, keepdims=True)
    scaled = (centred * scale_ref[...]).astype(jnp.bfloat16)
    projected = jnp.dot(w_ref[...], scaled, preferred_element_type=jnp.float32)
    out_ref[0:PATCHC, :] = projected.astype(jnp.bfloat16)
    rows = split3(average) + split3(squares)
    spare = jnp.zeros((PACK - PATCHC - len(rows), average.shape[1]), jnp.float32)
    out_ref[PATCHC:PACK, :] = jnp.concatenate(rows + [spare], axis=0).astype(jnp.bfloat16)


def project_values(weights, totals, value_pieces, scale_column, weight_rows):
    blocks, heads, keys, block = weights.shape
    width = heads * HD
    return pl.pallas_call(
        functools.partial(values_kernel, len(value_pieces), heads),
        grid=(blocks,),
        in_specs=[
            pl.BlockSpec((1, heads, keys, block), lambda i: (i, 0, 0, 0)),
            pl.BlockSpec((1, heads, block), lambda i: (i, 0, 0)),
            pl.BlockSpec((width, 1), lambda i: (0, 0)),
            pl.BlockSpec((PATCHC, width), lambda i: (0, 0)),
        ]
        + [pl.BlockSpec(v.shape, lambda i: (0, 0)) for v in value_pieces],
        out_specs=pl.BlockSpec((PACK, block), lambda i: (0, i)),
        out_shape=jax.ShapeDtypeStruct((PACK, blocks * block), jnp.bfloat16),
        name="values",
    )(weights, totals, scale_column, weight_rows, *value_pieces)


def merge_kernel(*refs):
    parts, out_ref = refs[:-1], refs[-1]
    tops = [part[0:PATCHC, :].astype(jnp.float32) for part in parts]
    out_ref[0:PATCHC, :] = sum(tops).astype(jnp.bfloat16)
    ends = [part[PATCHC:PACK, :].astype(jnp.float32) for part in parts]
    squares = sum(end[3:4] + end[4:5] + end[5:6] for end in ends)
    rows = [end[0:3] for end in ends] + split3(squares)
    used = 3 * len(parts) + 3
    rows.append(jnp.zeros((PACK - PATCHC - used, squares.shape[1]), jnp.float32))
    out_ref[PATCHC:PACK, :] = jnp.concatenate(rows, axis=0).astype(jnp.bfloat16)


def merge_parts(parts):
    return pl.pallas_call(
        merge_kernel,
        out_shape=jax.ShapeDtypeStruct(parts[0].shape, jnp.bfloat16),
        name="merge",
    )(*parts)


def finish_kernel(groups, width, tilt_ref, offset_ref, *refs):
    parts, out_ref = refs[:-1], refs[-1]
    ends = [part[PATCHC:PACK, :].astype(jnp.float32) for part in parts]
    means = []
    squares = 0.0
    for end in ends:
        for e in range(groups):
            means.append(end[3 * e : 3 * e + 1] + end[3 * e + 1 : 3 * e + 2] + end[3 * e + 2 : 3 * e + 3])
        base = 3 * groups
        squares = squares + end[base : base + 1] + end[base + 1 : base + 2] + end[base + 2 : base + 3]
    means = jnp.concatenate(means, axis=0)
    count = means.shape[0]
    average = jnp.sum(means, axis=0, keepdims=True) * (1.0 / count)
    away = means - average
    squares = squares + width * jnp.sum(away * away, axis=0, keepdims=True)
    inverse = lax.rsqrt(squares * (1.0 / (width * count)) + epsilon)
    top = sum(part[0:PATCHC, :].astype(jnp.float32) for part in parts)
    top = top + jnp.dot(
        tilt_ref[...], away, preferred_element_type=jnp.float32, precision=lax.Precision.HIGHEST
    )
    out_ref[...] = (top * inverse + offset_ref[...]).astype(jnp.bfloat16)


def finish_latents(parts, groups, width, tilt, offset):
    return pl.pallas_call(
        functools.partial(finish_kernel, groups, float(width)),
        out_shape=jax.ShapeDtypeStruct((PATCHC, parts[0].shape[1]), jnp.bfloat16),
        name="finish",
    )(tilt, offset, *parts)


def decode_kernel(tiles, past_ref, now_ref, pick_ref, inside_ref, spread_ref, centre_ref, w_ref, bias_ref, out_ref, pad_ref):
    patches = now_ref.shape[1] // CT
    pixels = 4 * TH * TW
    row_length = 2 * TW
    total = tiles * pixels
    frames = [(past_ref, f) for f in range(CT)] + [(now_ref, f) for f in range(CT)]
    sides = []
    for ab in range(PATCHC // LAT):
        side = [
            ref[ab * LAT : (ab + 1) * LAT, f * patches : (f + 1) * patches] for ref, f in frames
        ]
        sides.append(jnp.concatenate(side + side, axis=0))
    source = jnp.concatenate(sides, axis=1)
    picked = lax.dot_general(pick_ref[...], source, NT, preferred_element_type=jnp.float32)
    framed = picked * spread_ref[...] + centre_ref[...]
    lanes = lax.broadcasted_iota(jnp.int32, framed.shape, 1)
    first = lax.axis_index("tp") == 0
    early = (lanes % (2 * CT * LAT)) < CT * LAT
    framed = jnp.where(jnp.logical_and(first, early), 0.0, framed) * inside_ref[...]
    framed = framed.astype(jnp.bfloat16).astype(jnp.float32)
    margin = pad_ref.shape[0] - total
    half = margin // 2
    pad_ref[0:half, :] = jnp.zeros((half, framed.shape[1]), jnp.float32)
    pad_ref[half + total :, :] = jnp.zeros((half, framed.shape[1]), jnp.float32)
    pad_ref[half : half + total, :] = framed
    rows = lax.broadcasted_iota(jnp.int32, framed.shape, 0)
    column = rows % row_length
    line = (rows // row_length) % (2 * TH)
    low = lanes < 2 * CT * LAT

    def shifted(step):
        dy, dx = step // 3 - 1, step % 3 - 1
        start = half + dy * row_length + dx
        value = pad_ref[start : start + total, :]
        y, x = line + dy, column + dx
        keep = (y >= 0) & (y < 2 * TH) & (x >= 0) & (x < row_length)
        return jnp.where(keep, value, 0.0)

    columns = []
    for pair in range(5):
        left = shifted(2 * pair)
        right = shifted(2 * pair + 1) if 2 * pair + 1 < 9 else jnp.zeros_like(left)
        columns.append(jnp.where(low, left, right).astype(jnp.bfloat16))
    stacked = jnp.concatenate(columns, axis=1)
    result = jnp.dot(stacked, w_ref[...], preferred_element_type=jnp.float32) + bias_ref[...]
    result = result.astype(jnp.bfloat16)
    channels = out_ref.shape[-1]
    for n in range(tiles):
        for f in range(CT):
            out_ref[n, f] = result[n * pixels : (n + 1) * pixels, f * channels : (f + 1) * channels]


def decode_tiles(past, now, pick, inside, spread, centre, weight, bias, tiles):
    channels = weight.shape[1] // CT
    pixels = 4 * TH * TW
    return pl.pallas_call(
        functools.partial(decode_kernel, tiles),
        out_shape=jax.ShapeDtypeStruct((tiles, CT, pixels, channels), jnp.bfloat16),
        scratch_shapes=[pltpu.VMEM((tiles * pixels + 64, 4 * CT * LAT), jnp.float32)],
        name="decode",
    )(past, now, pick, inside, spread, centre, weight, bias)


def conv_operand(conv_weight):
    channels = conv_weight.shape[1]
    taps = conv_weight.reshape(3, 9, LAT, channels).transpose(1, 0, 2, 3)
    frames = []
    for f in range(CT):
        frames.append(jnp.pad(taps, ((0, 0), (f, CT - 1 - f), (0, 0), (0, 0))))
    stacked = jnp.concatenate(frames, axis=-1).reshape(9 * 2 * CT * LAT, CT * channels)
    return jnp.pad(stacked, ((0, 2 * CT * LAT), (0, 0)))


def pick_operand(tile_lists, patch_count):
    tiles = tile_lists.shape[0]
    grid = tile_lists.reshape(tiles, TH, 1, TW, 1)
    grid = jnp.broadcast_to(grid, (tiles, TH, 2, TW, 2)).reshape(-1, 1)
    pixel = jnp.arange(tiles * 4 * TILE_P)
    side = 2 * ((pixel // (2 * TW)) % 2) + pixel % 2
    lane = jnp.arange(4 * patch_count)
    match = (grid == (lane % patch_count)[None, :]) & (side[:, None] == (lane // patch_count)[None, :])
    return match.astype(jnp.bfloat16), (grid < patch_count).astype(jnp.float32)


def shards(
    queries,
    key_rows,
    value_rows,
    mod_scale,
    mod_shift,
    head_weight,
    tile_lists,
    latent_mean,
    latent_std,
    conv_weight,
    conv_bias,
):
    seq_count, tp_count = lax.axis_size("seq"), lax.axis_size("tp")
    seq, tp = lax.axis_index("seq"), lax.axis_index("tp")
    width = queries.shape[2]
    own_rows = queries.shape[1]
    split = (width // HD) % (seq_count * tp_count) == 0
    seq_width = width // seq_count
    parts = tp_count if split else 1
    part = tp if split else 0
    group_width = seq_width // parts
    patch_count = seq_count * WP

    def group_column(s, t):
        return (s * parts + t) * group_width

    query, key, value = queries[0], key_rows[0], value_rows[0]
    q_send = [
        lax.dynamic_slice_in_dim(query, (seq ^ d) * seq_width, seq_width, 1)
        for d in range(seq_count)
    ]
    k_send = [
        lax.dynamic_slice_in_dim(key, group_column(seq ^ d, part), group_width, 1)
        for d in range(seq_count)
    ]
    v_send = [
        lax.dynamic_slice_in_dim(value, group_column(seq ^ d, part), group_width, 1)
        for d in range(seq_count)
    ]

    def over_seq(pieces):
        order = sorted(range(1, seq_count), reverse=True)
        got = {0: pieces[0]}
        for d in order:
            got[d] = xor_permute(pieces[d], "seq", d)
        return [got[d] for d in range(seq_count)]

    q_got = over_seq(q_send)
    k_got = over_seq(k_send)
    stacked = jnp.stack(q_got)
    ordered = jnp.concatenate(
        [lax.dynamic_slice_in_dim(stacked, seq ^ s, 1, 0) for s in range(seq_count)], axis=0
    )
    ordered = ordered.reshape(seq_count, CT, WP, seq_width).transpose(1, 0, 2, 3)
    ordered = ordered.reshape(seq_count * own_rows, seq_width)
    if split:
        q_all = []
        for e in range(parts):
            piece = lax.dynamic_slice_in_dim(ordered, (tp ^ e) * group_width, group_width, 1)
            q_all.append(xor_permute(piece, "tp", e) if e else piece)
        q_all = jnp.concatenate(q_all, axis=0)
    else:
        q_all = ordered
    v_got = over_seq(v_send)

    gain = 1.0 + mod_scale[0]
    weight = head_weight.astype(jnp.float32)
    tilt_all = jnp.sum(
        (weight * gain[:, None]).reshape(seq_count * parts, group_width, PATCHC), axis=1
    )
    offset = jnp.sum(weight * mod_shift[0][:, None], axis=0)[:, None]
    start = group_column(seq, part)
    scale_column = lax.dynamic_slice_in_dim(gain, start, group_width, 0)[:, None]
    weight_rows = lax.dynamic_slice_in_dim(head_weight, start, group_width, 0).T
    block = math.gcd(seq_count * own_rows, 256)
    weights, totals = score_weights(q_all, k_got, block)
    packed = project_values(weights, totals, v_got, scale_column, weight_rows)

    tokens = seq_count * own_rows
    if seq_count * parts <= 16 and split:
        pieces = [packed[:, e * tokens : (e + 1) * tokens] for e in range(parts)]
        got = [pieces[0]] + [None] * (parts - 1)
        for e in range(parts - 1, 0, -1):
            got[e] = xor_permute(pieces[e], "tp", e)
        merged = merge_parts(got)
        across = [merged] + [None] * (seq_count - 1)
        for d in range(seq_count - 1, 0, -1):
            across[d] = xor_permute(merged, "seq", d)
        places = jnp.array(
            [[d, e] for d in range(seq_count) for e in range(parts)], jnp.int32
        )
        tilt = jnp.take(tilt_all, (places[:, 0] ^ seq) * parts + (places[:, 1] ^ tp), axis=0).T
        latent = finish_latents(across, parts, group_width, tilt, offset)
    else:
        stats = packed[PATCHC:].astype(jnp.float32)
        own_mean = stats[0:1] + stats[1:2] + stats[2:3]
        squares = stats[3:4] + stats[4:5] + stats[5:6]
        top = packed[:PATCHC].astype(jnp.float32)
        names = ("seq", "tp") if split else "seq"
        count = seq_count * parts
        average = lax.psum(own_mean, names) / count
        away = own_mean - average
        tilt = lax.dynamic_slice_in_dim(tilt_all, seq * parts + part, 1, 0).T
        squares = lax.psum(squares + group_width * away * away, names)
        top = lax.psum(top + tilt * away, names)
        inverse = lax.rsqrt(squares / width + epsilon)
        latent = (top * inverse + offset).astype(jnp.bfloat16)

    own = latent.reshape(PATCHC, CT, seq_count, WP)
    own = lax.dynamic_slice_in_dim(own, seq, 1, 2).reshape(PATCHC, own_rows).T

    def device(g, s, t):
        return (g * seq_count + s) * tp_count + t

    places = [(s, t) for s in range(seq_count) for t in range(tp_count)]
    names = ("segment", "seq", "tp")
    past = lax.ppermute(
        latent,
        names,
        [
            (device(g, s, t), device(1 - g, s, t + 1))
            for g in range(2)
            for s, t in places
            if t + 1 < tp_count
        ],
    )
    now = xor_permute(latent, "segment", 1)

    pick, inside = pick_operand(tile_lists, patch_count)
    spread = jnp.tile(latent_std, 4 * CT)[None, :]
    centre = jnp.tile(latent_mean, 4 * CT)[None, :]
    bias = jnp.tile(conv_bias, CT)[None, :]
    result = decode_tiles(
        past, now, pick, inside, spread, centre, conv_operand(conv_weight), bias, tile_lists.shape[0]
    )
    return (own[None], result[None])


def solution(mesh):
    in_specs = (
        P("segment", ("seq", "tp"), None),
        P("segment", "seq", None),
        P("segment", "seq", None),
        P("segment", None),
        P("segment", None),
        P(),
        P("seq", None),
        P(),
        P(),
        P(),
        P(),
    )
    out_specs = (P("segment", ("seq", "tp"), None), P("segment", "seq", "tp", None, None))
    return jax.shard_map(shards, mesh=mesh, in_specs=in_specs, out_specs=out_specs, check_vma=False)
```

```python
import functools
import math

import jax
import jax.numpy as jnp
from jax import lax
from jax.experimental import pallas as pl
from jax.experimental.pallas import tpu as pltpu
from jax.sharding import PartitionSpec as P

HD = 128
LAT = 16
PATCHC = 64
CT = 2
WP = 32
TH = 4
TW = 8
TILE_P = 32
PACK = 80

LIMIT = 24 << 20

epsilon = 1e-06


NT = (((1,), (1,)), ((), ()))
TN = (((0,), (0,)), ((), ()))


def xor_permute(value, axis, mask):
    pairs = [(i, i ^ mask) for i in range(lax.axis_size(axis))]
    return lax.ppermute(value, axis, pairs)


def split3(value):
    high = value.astype(jnp.bfloat16)
    rest = value - high.astype(jnp.float32)
    middle = rest.astype(jnp.bfloat16)
    low = (rest - middle.astype(jnp.float32)).astype(jnp.bfloat16)
    return [high.astype(jnp.float32), middle.astype(jnp.float32), low.astype(jnp.float32)]


def in_vmem(value):
    return pltpu.with_memory_space_constraint(value, pltpu.VMEM)


def vmem_call(kernel, outputs, name, *args):
    return pl.pallas_call(
        kernel,
        in_specs=[pl.BlockSpec(memory_space=pltpu.VMEM)] * len(args),
        out_specs=[pl.BlockSpec(memory_space=pltpu.VMEM)] * len(outputs),
        out_shape=[pltpu.VMEM(shape, dtype) for shape, dtype in outputs],
        compiler_params=pltpu.CompilerParams(vmem_limit_bytes=LIMIT),
        name=name,
    )(*[in_vmem(arg) for arg in args])


def softmax_block(query, k_refs, columns, store):
    factor = HD ** (-0.5) * math.log2(math.e)
    scores = [
        lax.dot_general(k[:, columns], query, NT, preferred_element_type=jnp.float32)
        for k in k_refs
    ]
    peak = functools.reduce(jnp.maximum, [jnp.max(x, axis=0, keepdims=True) for x in scores])
    total = 0.0
    for i, x in enumerate(scores):
        powers = jnp.exp2((x - peak) * factor)
        total = total + jnp.sum(powers, axis=0, keepdims=True)
        store(slice(i * x.shape[0], (i + 1) * x.shape[0]), powers.astype(jnp.bfloat16))
    return total


def project_block(mixed, scale_column, weight_rows):
    attended = jnp.concatenate(mixed, axis=0)
    average = jnp.sum(attended, axis=0, keepdims=True) * (1.0 / attended.shape[0])
    centred = attended - average
    squares = jnp.sum(centred * centred, axis=0, keepdims=True)
    scaled = (centred * scale_column).astype(jnp.bfloat16)
    projected = jnp.dot(weight_rows, scaled, preferred_element_type=jnp.float32)
    rows = split3(average) + split3(squares)
    spare = jnp.zeros((PACK - PATCHC - len(rows), average.shape[1]), jnp.float32)
    ends = jnp.concatenate(rows + [spare], axis=0)
    return projected.astype(jnp.bfloat16), ends.astype(jnp.bfloat16)


def scores_kernel(pieces, parts, heads, *refs):
    q_refs, k_refs, (p_ref, l_ref) = refs[:parts], refs[parts : parts + pieces], refs[parts + pieces :]
    for e in range(parts):
        for head in range(heads):
            columns = slice(head * HD, (head + 1) * HD)

            def store(rows, value):
                p_ref[e, head, rows, :] = value

            total = softmax_block(q_refs[e][:, columns], k_refs, columns, store)
            l_ref[e, head : head + 1, :] = total


def values_kernel(pieces, parts, heads, p_ref, l_ref, scale_ref, w_ref, *refs):
    v_refs, out_refs = refs[:pieces], refs[pieces:]
    size = v_refs[0].shape[0]
    for e in range(parts):
        mixed = []
        for head in range(heads):
            columns = slice(head * HD, (head + 1) * HD)
            total = 0.0
            for i, v in enumerate(v_refs):
                weights = p_ref[e, head, i * size : (i + 1) * size, :]
                total = total + lax.dot_general(
                    v[:, columns], weights, TN, preferred_element_type=jnp.float32
                )
            total = total / l_ref[e, head : head + 1, :]
            mixed.append(total.astype(jnp.bfloat16).astype(jnp.float32))
        top, ends = project_block(mixed, scale_ref[...], w_ref[...])
        out_refs[e][0:PATCHC, :] = top
        out_refs[e][PATCHC:PACK, :] = ends


def attend_resident(q_pieces, k_pieces, v_pieces, scale_column, weight_rows):
    parts, pieces = len(q_pieces), len(k_pieces)
    tokens, width = q_pieces[0].shape
    heads = width // HD
    keys = sum(k.shape[0] for k in k_pieces)
    weights, totals = vmem_call(
        functools.partial(scores_kernel, pieces, parts, heads),
        [((parts, heads, keys, tokens), jnp.bfloat16), ((parts, heads, tokens), jnp.float32)],
        "scores",
        *q_pieces,
        *k_pieces,
    )
    return vmem_call(
        functools.partial(values_kernel, pieces, parts, heads),
        [((PACK, tokens), jnp.bfloat16)] * parts,
        "values",
        weights,
        totals,
        scale_column,
        weight_rows,
        *v_pieces,
    )


def stream_kernel(heads, q_ref, k_ref, v_ref, scale_ref, w_ref, out_ref, p_ref):
    mixed = []
    for head in range(heads):
        columns = slice(head * HD, (head + 1) * HD)

        def store(rows, value):
            p_ref[rows, :] = value

        total = softmax_block(q_ref[:, columns], [k_ref], columns, store)
        value = lax.dot_general(
            v_ref[:, columns], p_ref[...], TN, preferred_element_type=jnp.float32
        )
        mixed.append((value / total).astype(jnp.bfloat16).astype(jnp.float32))
    top, ends = project_block(mixed, scale_ref[...], w_ref[...])
    out_ref[0:PATCHC, :] = top
    out_ref[PATCHC:PACK, :] = ends


def attend_streamed(query, key, value, scale_column, weight_rows):
    rows, width = query.shape
    block = math.gcd(rows, 256)
    keys = key.shape[0]

    def fixed(array):
        return pl.BlockSpec(array.shape, lambda i: (0, 0))

    return pl.pallas_call(
        functools.partial(stream_kernel, width // HD),
        grid=(rows // block,),
        in_specs=[pl.BlockSpec((block, width), lambda i: (i, 0))]
        + [fixed(key), fixed(value), fixed(scale_column), fixed(weight_rows)],
        out_specs=pl.BlockSpec((PACK, block), lambda i: (0, i)),
        out_shape=jax.ShapeDtypeStruct((PACK, rows), jnp.bfloat16),
        scratch_shapes=[pltpu.VMEM((keys, block), jnp.bfloat16)],
        name="attend",
    )(query, key, value, scale_column, weight_rows)


def merge_kernel(*refs):
    parts, out_ref = refs[:-1], refs[-1]
    tops = [part[0:PATCHC, :].astype(jnp.float32) for part in parts]
    out_ref[0:PATCHC, :] = sum(tops).astype(jnp.bfloat16)
    ends = [part[PATCHC:PACK, :].astype(jnp.float32) for part in parts]
    squares = sum(end[3:4] + end[4:5] + end[5:6] for end in ends)
    rows = [end[0:3] for end in ends] + split3(squares)
    used = 3 * len(parts) + 3
    rows.append(jnp.zeros((PACK - PATCHC - used, squares.shape[1]), jnp.float32))
    out_ref[PATCHC:PACK, :] = jnp.concatenate(rows, axis=0).astype(jnp.bfloat16)


def finish_kernel(groups, width, tilt_ref, offset_ref, *refs):
    parts, out_ref = refs[:-1], refs[-1]
    ends = [part[PATCHC:PACK, :].astype(jnp.float32) for part in parts]
    means = []
    squares = 0.0
    for end in ends:
        for row in range(0, 3 * groups, 3):
            means.append(end[row : row + 1] + end[row + 1 : row + 2] + end[row + 2 : row + 3])
        row = 3 * groups
        squares = squares + end[row : row + 1] + end[row + 1 : row + 2] + end[row + 2 : row + 3]
    means = jnp.concatenate(means, axis=0)
    count = means.shape[0]
    average = jnp.sum(means, axis=0, keepdims=True) * (1.0 / count)
    away = means - average
    squares = squares + width * jnp.sum(away * away, axis=0, keepdims=True)
    inverse = lax.rsqrt(squares * (1.0 / (width * count)) + epsilon)
    top = sum(part[0:PATCHC, :].astype(jnp.float32) for part in parts)
    top = top + jnp.dot(
        tilt_ref[...], away, preferred_element_type=jnp.float32, precision=lax.Precision.HIGHEST
    )
    out_ref[...] = (top * inverse + offset_ref[...]).astype(jnp.bfloat16)


def decode_kernel(tiles, past_ref, now_ref, pick_ref, inside_ref, affine_ref, w_ref, bias_ref, out_ref, pad_ref, result_ref, sem):
    patches = now_ref.shape[1] // CT
    pixels = 4 * TH * TW
    row_length = 2 * TW
    total = tiles * pixels
    frames = [(past_ref, f) for f in range(CT)] + [(now_ref, f) for f in range(CT)]
    sides = []
    for ab in range(PATCHC // LAT):
        side = [
            ref[ab * LAT : (ab + 1) * LAT, f * patches : (f + 1) * patches] for ref, f in frames
        ]
        sides.append(jnp.concatenate(side + side, axis=0))
    source = jnp.concatenate(sides, axis=1)
    picked = lax.dot_general(pick_ref[...], source, NT, preferred_element_type=jnp.float32)
    framed = picked * affine_ref[0:1, :] + affine_ref[1:2, :]
    lanes = lax.broadcasted_iota(jnp.int32, framed.shape, 1)
    first = lax.axis_index("tp") == 0
    early = (lanes % (2 * CT * LAT)) < CT * LAT
    drop = jnp.logical_or(jnp.logical_and(first, early), inside_ref[...] == 0.0)
    framed = jnp.where(drop, 0.0, framed)
    framed = framed.astype(jnp.bfloat16).astype(jnp.float32)
    half = (pad_ref.shape[0] - total) // 2
    pad_ref[0:half, :] = jnp.zeros((half, framed.shape[1]), jnp.float32)
    pad_ref[half + total :, :] = jnp.zeros((half, framed.shape[1]), jnp.float32)
    pad_ref[half : half + total, :] = framed
    shape = (pixels, framed.shape[1])
    rows = lax.broadcasted_iota(jnp.int32, shape, 0)
    column = rows % row_length
    line = rows // row_length
    low = lax.broadcasted_iota(jnp.int32, shape, 1) < 2 * CT * LAT
    channels = out_ref.shape[-1]
    copies = []
    for n in range(tiles):

        def shifted(step):
            dy, dx = step // 3 - 1, step % 3 - 1
            start = half + n * pixels + dy * row_length + dx
            value = pad_ref[start : start + pixels, :]
            y, x = line + dy, column + dx
            keep = (y >= 0) & (y < 2 * TH) & (x >= 0) & (x < row_length)
            return jnp.where(keep, value, 0.0)

        columns = []
        for pair in range(5):
            left = shifted(2 * pair)
            right = shifted(2 * pair + 1) if 2 * pair + 1 < 9 else jnp.zeros_like(left)
            columns.append(jnp.where(low, left, right).astype(jnp.bfloat16))
        stacked = jnp.concatenate(columns, axis=1)
        result = jnp.dot(stacked, w_ref[...], preferred_element_type=jnp.float32) + bias_ref[...]
        result = result.astype(jnp.bfloat16)
        for f in range(CT):
            result_ref[n, f] = result[:, f * channels : (f + 1) * channels]
        copy = pltpu.make_async_copy(result_ref.at[n], out_ref.at[n], sem.at[n])
        copy.start()
        copies.append(copy)
    for copy in copies:
        copy.wait()


def decode_tiles(past, now, pick, inside, affine, weight, bias, tiles):
    channels = weight.shape[1] // CT
    pixels = 4 * TH * TW
    args = [past, now, pick, inside, affine, weight, bias]
    shape = (tiles, CT, pixels, channels)
    return pl.pallas_call(
        functools.partial(decode_kernel, tiles),
        in_specs=[pl.BlockSpec(memory_space=pltpu.VMEM)] * len(args),
        out_specs=pl.BlockSpec(memory_space=pl.ANY),
        out_shape=jax.ShapeDtypeStruct(shape, jnp.bfloat16),
        scratch_shapes=[
            pltpu.VMEM((tiles * pixels + 64, 4 * CT * LAT), jnp.float32),
            pltpu.VMEM(shape, jnp.bfloat16),
            pltpu.SemaphoreType.DMA((tiles,)),
        ],
        compiler_params=pltpu.CompilerParams(vmem_limit_bytes=LIMIT),
        name="decode",
    )(*[in_vmem(arg) for arg in args])


def conv_operand(conv_weight):
    channels = conv_weight.shape[1]
    taps = conv_weight.reshape(3, 9, LAT, channels).transpose(1, 0, 2, 3)
    frames = []
    for f in range(CT):
        frames.append(jnp.pad(taps, ((0, 0), (f, CT - 1 - f), (0, 0), (0, 0))))
    stacked = jnp.concatenate(frames, axis=-1).reshape(9 * 2 * CT * LAT, CT * channels)
    return jnp.pad(stacked, ((0, 2 * CT * LAT), (0, 0)))


def pick_operand(tile_lists, patch_count):
    tiles = tile_lists.shape[0]
    grid = tile_lists.reshape(tiles, TH, 1, TW, 1)
    grid = jnp.broadcast_to(grid, (tiles, TH, 2, TW, 2)).reshape(-1, 1)
    pixel = jnp.arange(tiles * 4 * TILE_P)
    side = 2 * ((pixel // (2 * TW)) % 2) + pixel % 2
    lane = jnp.arange(4 * patch_count)
    match = (grid == (lane % patch_count)[None, :]) & (side[:, None] == (lane // patch_count)[None, :])
    return match.astype(jnp.bfloat16), (grid < patch_count).astype(jnp.float32)


def shards(
    queries,
    key_rows,
    value_rows,
    mod_scale,
    mod_shift,
    head_weight,
    tile_lists,
    latent_mean,
    latent_std,
    conv_weight,
    conv_bias,
):
    seq_count, tp_count = lax.axis_size("seq"), lax.axis_size("tp")
    seq, tp = lax.axis_index("seq"), lax.axis_index("tp")
    width = queries.shape[2]
    own_rows = queries.shape[1]
    split = (width // HD) % (seq_count * tp_count) == 0
    seq_width = width // seq_count
    parts = tp_count if split else 1
    part = tp if split else 0
    group_width = seq_width // parts
    patch_count = seq_count * WP

    def group_column(s, t):
        return (s * parts + t) * group_width

    query, key, value = queries[0], key_rows[0], value_rows[0]
    q_send = [
        lax.dynamic_slice_in_dim(query, (seq ^ d) * seq_width, seq_width, 1)
        for d in range(seq_count)
    ]
    k_send = [
        lax.dynamic_slice_in_dim(key, group_column(seq ^ d, part), group_width, 1)
        for d in range(seq_count)
    ]
    v_send = [
        lax.dynamic_slice_in_dim(value, group_column(seq ^ d, part), group_width, 1)
        for d in range(seq_count)
    ]

    def over_seq(pieces):
        order = sorted(range(1, seq_count), reverse=True)
        got = {0: pieces[0]}
        for d in order:
            got[d] = xor_permute(pieces[d], "seq", d)
        return [got[d] for d in range(seq_count)]

    mods = jnp.concatenate([mod_scale, mod_shift], axis=0)
    far_mods = xor_permute(mods, "segment", 1)
    q_got = over_seq(q_send)
    k_got = over_seq(k_send)
    stacked = jnp.stack(q_got)
    ordered = jnp.concatenate(
        [lax.dynamic_slice_in_dim(stacked, seq ^ s, 1, 0) for s in range(seq_count)], axis=0
    )
    ordered = ordered.reshape(seq_count, CT, WP, seq_width).transpose(1, 0, 2, 3)
    ordered = ordered.reshape(seq_count * own_rows, seq_width)
    q_send = [
        lax.dynamic_slice_in_dim(ordered, (part ^ e) * group_width, group_width, 1)
        for e in range(parts)
    ]
    q_send, v_send = lax.optimization_barrier((q_send, v_send))
    q_all = [q_send[0]] + [None] * (parts - 1)
    for e in range(parts - 1, 0, -1):
        q_all[e] = xor_permute(q_send[e], "tp", e)
    v_got = over_seq(v_send)

    start = group_column(seq, part)
    scale_column = lax.dynamic_slice_in_dim(1.0 + mod_scale[0], start, group_width, 0)[:, None]
    weight_rows = lax.dynamic_slice_in_dim(head_weight, start, group_width, 0).T
    weight = head_weight.astype(jnp.float32)
    far_gain = 1.0 + far_mods[0]
    tilt_all = jnp.sum(
        (weight * far_gain[:, None]).reshape(seq_count * parts, group_width, PATCHC), axis=1
    )
    offset = jnp.sum(weight * far_mods[1][:, None], axis=0)[:, None]
    places = jnp.array([[d, e] for d in range(seq_count) for e in range(parts)], jnp.int32)
    tilt = jnp.take(tilt_all, (places[:, 0] ^ seq) * parts + (places[:, 1] ^ part), axis=0).T
    pick, inside = pick_operand(tile_lists, patch_count)
    affine = jnp.stack([jnp.tile(latent_std, 4 * CT), jnp.tile(latent_mean, 4 * CT)])
    bias = jnp.tile(conv_bias, CT)[None, :]
    conv = conv_operand(conv_weight)
    q_all, (scale_column, weight_rows, tilt, offset, pick, inside, affine, bias, conv) = (
        lax.optimization_barrier(
            (q_all, (scale_column, weight_rows, tilt, offset, pick, inside, affine, bias, conv))
        )
    )

    def device(g, s, t):
        return (g * seq_count + s) * tp_count + t

    places = [(g, s, t) for g in range(2) for s in range(seq_count) for t in range(tp_count)]
    names = ("segment", "seq", "tp")

    def across(value, e):
        pairs = [(device(g, s, t), device(1 - g, s, t ^ e)) for g, s, t in places]
        return lax.ppermute(value, names, pairs)

    if split and seq_count * parts <= 16:
        pieces = attend_resident(q_all, k_got, v_got, scale_column, weight_rows)
        got = [None] * parts
        for e in range(parts - 1, -1, -1):
            got[e] = across(pieces[e], e)
        shape = got[0].shape
        (merged,) = vmem_call(merge_kernel, [(shape, jnp.bfloat16)], "merge", *got)
        spread = [merged] + [None] * (seq_count - 1)
        for d in range(seq_count - 1, 0, -1):
            spread[d] = xor_permute(merged, "seq", d)
        (latent,) = vmem_call(
            functools.partial(finish_kernel, parts, float(group_width)),
            [((PATCHC, shape[1]), jnp.bfloat16)],
            "finish",
            tilt,
            offset,
            *spread,
        )
    else:
        packed = attend_streamed(
            jnp.concatenate(q_all, axis=0),
            jnp.concatenate(k_got, axis=0),
            jnp.concatenate(v_got, axis=0),
            scale_column,
            weight_rows,
        )
        tokens = seq_count * own_rows
        got = [across(packed[:, e * tokens : (e + 1) * tokens], e) for e in range(parts)]
        top = squares = 0.0
        means = []
        for piece in got:
            ends = piece[PATCHC:].astype(jnp.float32)
            means.append(ends[0:1] + ends[1:2] + ends[2:3])
            squares = squares + ends[3:4] + ends[4:5] + ends[5:6]
            top = top + piece[:PATCHC].astype(jnp.float32)
        average = lax.psum(sum(means), "seq") / (seq_count * parts)
        for e, mean in enumerate(means):
            away = mean - average
            squares = squares + group_width * away * away
            top = top + tilt[:, e : e + 1] * away
        squares = lax.psum(squares, "seq")
        top = lax.psum(top, "seq")
        inverse = lax.rsqrt(squares / width + epsilon)
        latent = (top * inverse + offset).astype(jnp.bfloat16)

    past = lax.ppermute(latent, "tp", [(t, t + 1) for t in range(tp_count - 1)])
    own = latent.reshape(PATCHC, CT, seq_count, WP)
    own = lax.dynamic_slice_in_dim(own, seq, 1, 2).reshape(PATCHC, own_rows).T
    own = xor_permute(own, "segment", 1)
    result = decode_tiles(past, latent, pick, inside, affine, conv, bias, tile_lists.shape[0])
    return (own[None], result[None])


def solution(mesh):
    in_specs = (
        P("segment", ("seq", "tp"), None),
        P("segment", "seq", None),
        P("segment", "seq", None),
        P("segment", None),
        P("segment", None),
        P(),
        P("seq", None),
        P(),
        P(),
        P(),
        P(),
    )
    out_specs = (P("segment", ("seq", "tp"), None), P("segment", "seq", "tp", None, None))
    return jax.shard_map(shards, mesh=mesh, in_specs=in_specs, out_specs=out_specs, check_vma=False)
```

```python
import functools
import math

import jax
import jax.numpy as jnp
from jax import lax
from jax.experimental import pallas as pl
from jax.experimental.pallas import tpu as pltpu
from jax.sharding import PartitionSpec as P


HD = 128
LAT = 16
PATCHC = 64
CT = 2
WP = 32
TH = 4
TW = 8
TILE_P = 32
PACK = 80

LIMIT = 24 << 20

epsilon = 1e-06


NT = (((1,), (1,)), ((), ()))
TN = (((0,), (0,)), ((), ()))


def xor_permute(value, axis, mask):
    pairs = [(i, i ^ mask) for i in range(lax.axis_size(axis))]
    return lax.ppermute(value, axis, pairs)


def split3(value):
    high = value.astype(jnp.bfloat16)
    rest = value - high.astype(jnp.float32)
    middle = rest.astype(jnp.bfloat16)
    low = (rest - middle.astype(jnp.float32)).astype(jnp.bfloat16)
    return [high.astype(jnp.float32), middle.astype(jnp.float32), low.astype(jnp.float32)]


def in_vmem(value):
    return pltpu.with_memory_space_constraint(value, pltpu.VMEM)


def vmem_call(kernel, outputs, *args):
    return pl.pallas_call(
        kernel,
        in_specs=[pl.BlockSpec(memory_space=pltpu.VMEM)] * len(args),
        out_specs=[pl.BlockSpec(memory_space=pltpu.VMEM)] * len(outputs),
        out_shape=[pltpu.VMEM(shape, dtype) for shape, dtype in outputs],
        compiler_params=pltpu.CompilerParams(vmem_limit_bytes=LIMIT),
    )(*[in_vmem(arg) for arg in args])


def softmax_block(query, k_refs, columns, store):
    factor = HD ** (-0.5) * math.log2(math.e)
    scores = [
        lax.dot_general(k[:, columns], query, NT, preferred_element_type=jnp.float32)
        for k in k_refs
    ]
    peak = functools.reduce(jnp.maximum, [jnp.max(x, axis=0, keepdims=True) for x in scores])
    total = 0.0
    for i, x in enumerate(scores):
        powers = jnp.exp2((x - peak) * factor)
        total = total + jnp.sum(powers, axis=0, keepdims=True)
        store(slice(i * x.shape[0], (i + 1) * x.shape[0]), powers.astype(jnp.bfloat16))
    return total


def scaled_weight(gain_row, weight_rows):
    scaled = weight_rows.astype(jnp.float32) * gain_row
    high = scaled.astype(jnp.bfloat16)
    low = (scaled - high.astype(jnp.float32)).astype(jnp.bfloat16)
    tilt = jnp.sum(high.astype(jnp.float32) + low.astype(jnp.float32), axis=1, keepdims=True)
    return jnp.concatenate([high, low], axis=0), tilt


def project_block(mixed, weight_pair, tilt):
    attended = jnp.concatenate(mixed, axis=0)
    values = attended.astype(jnp.float32)
    average = jnp.sum(values, axis=0, keepdims=True) * (1.0 / values.shape[0])
    centred = values - average
    squares = jnp.sum(centred * centred, axis=0, keepdims=True)
    both = jnp.dot(weight_pair, attended, preferred_element_type=jnp.float32)
    projected = both[:PATCHC] + both[PATCHC:] - tilt * average
    rows = split3(average) + split3(squares)
    spare = jnp.zeros((PACK - PATCHC - len(rows), average.shape[1]), jnp.float32)
    ends = jnp.concatenate(rows + [spare], axis=0)
    return projected.astype(jnp.bfloat16), ends.astype(jnp.bfloat16)


def scores_kernel(pieces, parts, heads, *refs):
    q_refs, k_refs, (p_ref, l_ref) = refs[:parts], refs[parts : parts + pieces], refs[parts + pieces :]
    for e in range(parts):
        for head in range(heads):
            columns = slice(head * HD, (head + 1) * HD)

            def store(rows, value):
                p_ref[e, head, rows, :] = value

            total = softmax_block(q_refs[e][:, columns], k_refs, columns, store)
            l_ref[e, head : head + 1, :] = total


def values_kernel(pieces, parts, heads, p_ref, l_ref, gain_ref, w_ref, *refs):
    v_refs, out_refs = refs[:pieces], refs[pieces:]
    pair, tilt = scaled_weight(gain_ref[...], w_ref[...])
    size = v_refs[0].shape[0]
    for e in range(parts):
        mixed = []
        for head in range(heads):
            columns = slice(head * HD, (head + 1) * HD)
            total = 0.0
            for i, v in enumerate(v_refs):
                weights = p_ref[e, head, i * size : (i + 1) * size, :]
                total = total + lax.dot_general(
                    v[:, columns], weights, TN, preferred_element_type=jnp.float32
                )
            total = total / l_ref[e, head : head + 1, :]
            mixed.append(total.astype(jnp.bfloat16))
        top, ends = project_block(mixed, pair, tilt)
        out_refs[e][0:PATCHC, :] = top
        out_refs[e][PATCHC:PACK, :] = ends


def attend_resident(q_pieces, k_pieces, v_pieces, gain_row, weight_rows):
    parts, pieces = len(q_pieces), len(k_pieces)
    tokens, width = q_pieces[0].shape
    heads = width // HD
    keys = sum(k.shape[0] for k in k_pieces)
    weights, totals = vmem_call(
        functools.partial(scores_kernel, pieces, parts, heads),
        [((parts, heads, keys, tokens), jnp.bfloat16), ((parts, heads, tokens), jnp.float32)],
        *q_pieces,
        *k_pieces,
    )
    return vmem_call(
        functools.partial(values_kernel, pieces, parts, heads),
        [((PACK, tokens), jnp.bfloat16)] * parts,
        weights,
        totals,
        gain_row,
        weight_rows,
        *v_pieces,
    )


def stream_kernel(heads, q_ref, k_ref, v_ref, gain_ref, w_ref, out_ref, p_ref):
    mixed = []
    for head in range(heads):
        columns = slice(head * HD, (head + 1) * HD)

        def store(rows, value):
            p_ref[rows, :] = value

        total = softmax_block(q_ref[:, columns], [k_ref], columns, store)
        value = lax.dot_general(
            v_ref[:, columns], p_ref[...], TN, preferred_element_type=jnp.float32
        )
        mixed.append((value / total).astype(jnp.bfloat16))
    top, ends = project_block(mixed, *scaled_weight(gain_ref[...], w_ref[...]))
    out_ref[0:PATCHC, :] = top
    out_ref[PATCHC:PACK, :] = ends


def attend_streamed(query, key, value, gain_row, weight_rows):
    rows, width = query.shape
    block = math.gcd(rows, 256)
    keys = key.shape[0]

    def fixed(array):
        return pl.BlockSpec(array.shape, lambda i: (0, 0))

    return pl.pallas_call(
        functools.partial(stream_kernel, width // HD),
        grid=(rows // block,),
        in_specs=[pl.BlockSpec((block, width), lambda i: (i, 0))]
        + [fixed(key), fixed(value), fixed(gain_row), fixed(weight_rows)],
        out_specs=pl.BlockSpec((PACK, block), lambda i: (0, i)),
        out_shape=jax.ShapeDtypeStruct((PACK, rows), jnp.bfloat16),
        scratch_shapes=[pltpu.VMEM((keys, block), jnp.bfloat16)],
        name="attend",
    )(query, key, value, gain_row, weight_rows)


def merge_kernel(*refs):
    parts, out_ref = refs[:-1], refs[-1]
    tops = [part[0:PATCHC, :].astype(jnp.float32) for part in parts]
    out_ref[0:PATCHC, :] = sum(tops).astype(jnp.bfloat16)
    ends = [part[PATCHC:PACK, :].astype(jnp.float32) for part in parts]
    squares = sum(end[3:4] + end[4:5] + end[5:6] for end in ends)
    rows = [end[0:3] for end in ends] + split3(squares)
    used = 3 * len(parts) + 3
    rows.append(jnp.zeros((PACK - PATCHC - used, squares.shape[1]), jnp.float32))
    out_ref[PATCHC:PACK, :] = jnp.concatenate(rows, axis=0).astype(jnp.bfloat16)


def finish_kernel(groups, width, tilt_ref, offset_ref, *refs):
    parts, out_ref = refs[:-1], refs[-1]
    ends = [part[PATCHC:PACK, :].astype(jnp.float32) for part in parts]
    means = []
    squares = 0.0
    for end in ends:
        for row in range(0, 3 * groups, 3):
            means.append(end[row : row + 1] + end[row + 1 : row + 2] + end[row + 2 : row + 3])
        row = 3 * groups
        squares = squares + end[row : row + 1] + end[row + 1 : row + 2] + end[row + 2 : row + 3]
    means = jnp.concatenate(means, axis=0)
    count = means.shape[0]
    average = jnp.sum(means, axis=0, keepdims=True) * (1.0 / count)
    away = means - average
    squares = squares + width * jnp.sum(away * away, axis=0, keepdims=True)
    inverse = lax.rsqrt(squares * (1.0 / (width * count)) + epsilon)
    top = sum(part[0:PATCHC, :].astype(jnp.float32) for part in parts)
    top = top + jnp.dot(
        tilt_ref[...], away, preferred_element_type=jnp.float32, precision=lax.Precision.HIGHEST
    )
    out_ref[...] = (top * inverse + offset_ref[...]).astype(jnp.bfloat16)


def decode_kernel(tiles, past_ref, now_ref, pick_ref, inside_ref, affine_ref, w_ref, bias_ref, out_ref, pad_ref, result_ref, sem):
    patches = now_ref.shape[1] // CT
    pixels = 4 * TH * TW
    row_length = 2 * TW
    total = tiles * pixels
    frames = [(past_ref, f) for f in range(CT)] + [(now_ref, f) for f in range(CT)]
    sides = []
    for ab in range(PATCHC // LAT):
        side = [
            ref[ab * LAT : (ab + 1) * LAT, f * patches : (f + 1) * patches] for ref, f in frames
        ]
        sides.append(jnp.concatenate(side + side, axis=0))
    source = jnp.concatenate(sides, axis=1)
    picked = lax.dot_general(pick_ref[...], source, NT, preferred_element_type=jnp.float32)
    framed = picked * affine_ref[0:1, :] + affine_ref[1:2, :]
    lanes = lax.broadcasted_iota(jnp.int32, framed.shape, 1)
    first = lax.axis_index("tp") == 0
    early = (lanes % (2 * CT * LAT)) < CT * LAT
    drop = jnp.logical_or(jnp.logical_and(first, early), inside_ref[...] == 0.0)
    framed = jnp.where(drop, 0.0, framed)
    framed = framed.astype(jnp.bfloat16).astype(jnp.float32)
    half = (pad_ref.shape[0] - total) // 2
    pad_ref[0:half, :] = jnp.zeros((half, framed.shape[1]), jnp.float32)
    pad_ref[half + total :, :] = jnp.zeros((half, framed.shape[1]), jnp.float32)
    pad_ref[half : half + total, :] = framed
    shape = (pixels, framed.shape[1])
    rows = lax.broadcasted_iota(jnp.int32, shape, 0)
    column = rows % row_length
    line = rows // row_length
    low = lax.broadcasted_iota(jnp.int32, shape, 1) < 2 * CT * LAT
    channels = out_ref.shape[-1]
    copies = []
    for n in range(tiles):

        def shifted(step):
            dy, dx = step // 3 - 1, step % 3 - 1
            start = half + n * pixels + dy * row_length + dx
            value = pad_ref[start : start + pixels, :]
            y, x = line + dy, column + dx
            keep = (y >= 0) & (y < 2 * TH) & (x >= 0) & (x < row_length)
            return jnp.where(keep, value, 0.0)

        columns = []
        for pair in range(5):
            left = shifted(2 * pair)
            right = shifted(2 * pair + 1) if 2 * pair + 1 < 9 else jnp.zeros_like(left)
            columns.append(jnp.where(low, left, right).astype(jnp.bfloat16))
        stacked = jnp.concatenate(columns, axis=1)
        result = jnp.dot(stacked, w_ref[...], preferred_element_type=jnp.float32) + bias_ref[...]
        result = result.astype(jnp.bfloat16)
        for f in range(CT):
            result_ref[n, f] = result[:, f * channels : (f + 1) * channels]
        copy = pltpu.make_async_copy(result_ref.at[n], out_ref.at[n], sem.at[n])
        copy.start()
        copies.append(copy)
    for copy in copies:
        copy.wait()


def decode_tiles(past, now, pick, inside, affine, weight, bias, tiles):
    channels = weight.shape[1] // CT
    pixels = 4 * TH * TW
    args = [past, now, pick, inside, affine, weight, bias]
    shape = (tiles, CT, pixels, channels)
    return pl.pallas_call(
        functools.partial(decode_kernel, tiles),
        in_specs=[pl.BlockSpec(memory_space=pltpu.VMEM)] * len(args),
        out_specs=pl.BlockSpec(memory_space=pl.ANY),
        out_shape=jax.ShapeDtypeStruct(shape, jnp.bfloat16),
        scratch_shapes=[
            pltpu.VMEM((tiles * pixels + 64, 4 * CT * LAT), jnp.float32),
            pltpu.VMEM(shape, jnp.bfloat16),
            pltpu.SemaphoreType.DMA((tiles,)),
        ],
        compiler_params=pltpu.CompilerParams(vmem_limit_bytes=LIMIT),
        name="decode",
    )(*[in_vmem(arg) for arg in args])


def conv_operand(conv_weight):
    channels = conv_weight.shape[1]
    taps = conv_weight.reshape(3, 9, LAT, channels).transpose(1, 0, 2, 3)
    frames = []
    for f in range(CT):
        frames.append(jnp.pad(taps, ((0, 0), (f, CT - 1 - f), (0, 0), (0, 0))))
    stacked = jnp.concatenate(frames, axis=-1).reshape(9 * 2 * CT * LAT, CT * channels)
    return jnp.pad(stacked, ((0, 2 * CT * LAT), (0, 0)))


def pick_operand(tile_lists, patch_count):
    tiles = tile_lists.shape[0]
    grid = tile_lists.reshape(tiles, TH, 1, TW, 1)
    grid = jnp.broadcast_to(grid, (tiles, TH, 2, TW, 2)).reshape(-1, 1)
    pixel = jnp.arange(tiles * 4 * TILE_P)
    side = 2 * ((pixel // (2 * TW)) % 2) + pixel % 2
    lane = jnp.arange(4 * patch_count)
    match = (grid == (lane % patch_count)[None, :]) & (side[:, None] == (lane // patch_count)[None, :])
    return match.astype(jnp.bfloat16), (grid < patch_count).astype(jnp.float32)


def run(
    queries,
    key_rows,
    value_rows,
    mod_scale,
    mod_shift,
    head_weight,
    tile_lists,
    latent_mean,
    latent_std,
    conv_weight,
    conv_bias,
):
    seq_count, tp_count = lax.axis_size("seq"), lax.axis_size("tp")
    seq, tp = lax.axis_index("seq"), lax.axis_index("tp")
    width = queries.shape[2]
    own_rows = queries.shape[1]
    split = (width // HD) % (seq_count * tp_count) == 0
    seq_width = width // seq_count
    parts = tp_count if split else 1
    part = tp if split else 0
    group_width = seq_width // parts
    patch_count = seq_count * WP

    def group_column(s, t):
        return (s * parts + t) * group_width

    query, key, value = queries[0], key_rows[0], value_rows[0]
    q_send = [
        lax.dynamic_slice_in_dim(query, (seq ^ d) * seq_width, seq_width, 1)
        for d in range(seq_count)
    ]
    k_send = [
        lax.dynamic_slice_in_dim(key, group_column(seq ^ d, part), group_width, 1)
        for d in range(seq_count)
    ]
    v_send = [
        lax.dynamic_slice_in_dim(value, group_column(seq ^ d, part), group_width, 1)
        for d in range(seq_count)
    ]

    def over_seq(pieces):
        order = sorted(range(1, seq_count), reverse=True)
        got = {0: pieces[0]}
        for d in order:
            got[d] = xor_permute(pieces[d], "seq", d)
        return [got[d] for d in range(seq_count)]

    q_got = over_seq(q_send)
    k_got = over_seq(k_send)
    v_got = over_seq(v_send)
    stacked = jnp.stack(q_got)
    ordered = jnp.concatenate(
        [lax.dynamic_slice_in_dim(stacked, seq ^ s, 1, 0) for s in range(seq_count)], axis=0
    )
    ordered = ordered.reshape(seq_count, CT, WP, seq_width).transpose(1, 0, 2, 3)
    ordered = ordered.reshape(seq_count * own_rows, seq_width)
    q_send = [
        lax.dynamic_slice_in_dim(ordered, (part ^ e) * group_width, group_width, 1)
        for e in range(parts)
    ]
    small = (mod_scale, mod_shift, head_weight, tile_lists, latent_mean, latent_std, conv_weight, conv_bias)
    q_send, small = lax.optimization_barrier((q_send, small))
    mod_scale, mod_shift, head_weight, tile_lists, latent_mean, latent_std, conv_weight, conv_bias = small
    q_all = [q_send[0]] + [None] * (parts - 1)
    for e in range(parts - 1, 0, -1):
        q_all[e] = xor_permute(q_send[e], "tp", e)
    far_mods = xor_permute(jnp.concatenate([mod_scale, mod_shift], axis=0), "segment", 1)

    start = group_column(seq, part)
    gain_row = 1.0 + lax.dynamic_slice_in_dim(mod_scale, start, group_width, 1)
    weight_rows = lax.dynamic_slice_in_dim(head_weight, start, group_width, 0).T
    weight = head_weight.astype(jnp.float32)
    far_gain = 1.0 + far_mods[0]
    tilt_all = jnp.sum(
        (weight * far_gain[:, None]).reshape(seq_count * parts, group_width, PATCHC), axis=1
    )
    offset = jnp.sum(weight * far_mods[1][:, None], axis=0)[:, None]
    places = jnp.array([[d, e] for d in range(seq_count) for e in range(parts)], jnp.int32)
    tilt = jnp.take(tilt_all, (places[:, 0] ^ seq) * parts + (places[:, 1] ^ part), axis=0).T
    pick, inside = pick_operand(tile_lists, patch_count)
    affine = jnp.stack([jnp.tile(latent_std, 4 * CT), jnp.tile(latent_mean, 4 * CT)])
    bias = jnp.tile(conv_bias, CT)[None, :]
    conv = conv_operand(conv_weight)
    ready = (gain_row, weight_rows, tilt, offset, pick, inside, affine, bias, conv)
    v_got, ready = lax.optimization_barrier((v_got, ready))
    gain_row, weight_rows, tilt, offset, pick, inside, affine, bias, conv = ready

    def device(g, s, t):
        return (g * seq_count + s) * tp_count + t

    places = [(g, s, t) for g in range(2) for s in range(seq_count) for t in range(tp_count)]
    names = ("segment", "seq", "tp")

    def across(value, e):
        pairs = [(device(g, s, t), device(1 - g, s, t ^ e)) for g, s, t in places]
        return lax.ppermute(value, names, pairs)

    if split and seq_count * parts <= 16:
        pieces = attend_resident(q_all, k_got, v_got, gain_row, weight_rows)
        got = [None] * parts
        for e in range(parts - 1, -1, -1):
            got[e] = across(pieces[e], e)
        shape = got[0].shape
        (merged,) = vmem_call(merge_kernel, [(shape, jnp.bfloat16)], *got)
        spread = [merged] + [None] * (seq_count - 1)
        for d in range(1, seq_count):
            spread[d] = xor_permute(merged, "seq", d)
        (latent,) = vmem_call(
            functools.partial(finish_kernel, parts, float(group_width)),
            [((PATCHC, shape[1]), jnp.bfloat16)],
            tilt,
            offset,
            *spread,
        )
    else:
        packed = attend_streamed(
            jnp.concatenate(q_all, axis=0),
            jnp.concatenate(k_got, axis=0),
            jnp.concatenate(v_got, axis=0),
            gain_row,
            weight_rows,
        )
        tokens = seq_count * own_rows
        got = [across(packed[:, e * tokens : (e + 1) * tokens], e) for e in range(parts)]
        top = squares = 0.0
        means = []
        for piece in got:
            ends = piece[PATCHC:].astype(jnp.float32)
            means.append(ends[0:1] + ends[1:2] + ends[2:3])
            squares = squares + ends[3:4] + ends[4:5] + ends[5:6]
            top = top + piece[:PATCHC].astype(jnp.float32)
        average = lax.psum(sum(means), "seq") / (seq_count * parts)
        for e, mean in enumerate(means):
            away = mean - average
            squares = squares + group_width * away * away
            top = top + tilt[:, e : e + 1] * away
        squares = lax.psum(squares, "seq")
        top = lax.psum(top, "seq")
        inverse = lax.rsqrt(squares / width + epsilon)
        latent = (top * inverse + offset).astype(jnp.bfloat16)

    past = lax.ppermute(latent, "tp", [(t, t + 1) for t in range(tp_count - 1)])
    own = latent.reshape(PATCHC, CT, seq_count, WP)
    own = lax.dynamic_slice_in_dim(own, seq, 1, 2).reshape(PATCHC, own_rows).T
    own = xor_permute(own, "segment", 1)
    result = decode_tiles(past, latent, pick, inside, affine, conv, bias, tile_lists.shape[0])
    return (own[None], result[None])


def solution(mesh):
    in_specs = (
        P("segment", ("seq", "tp"), None),
        P("segment", "seq", None),
        P("segment", "seq", None),
        P("segment", None),
        P("segment", None),
        P(),
        P("seq", None),
        P(),
        P(),
        P(),
        P(),
    )
    out_specs = (P("segment", ("seq", "tp"), None), P("segment", "seq", "tp", None, None))
    return jax.shard_map(run, mesh=mesh, in_specs=in_specs, out_specs=out_specs, check_vma=False)
```
